32 devices in a mesh: grp: 2 (over x), ctr: 16 (over z, y, core).
Axes of the slice: x: 2, y: 2, z: 4, core: 2. Of those that a mesh axis runs over, the one named last changes fastest.
Arguments:
- centres: bfloat16 [6144, 768], P(('grp', 'ctr')), parts along dimension 0
- sample_idx: int32 [1024], P(('grp', 'ctr')), parts along dimension 0, may hold values from 0 to 3071, as said below
- coef: float32 [6144], P(('grp', 'ctr')), parts along dimension 0
- metric_factor: bfloat16 [768, 768], replicated, may hold values from -0.21875 to 0.21875
Outputs:
- metric_new: float32 [1536, 768], P(('grp', 'ctr')), parts along dimension 0
- transformed: float32 [1024, 768], P(('grp', 'ctr')), parts along dimension 0
The draws below stay inside these ranges and needn't reach their ends.
There are 2 independent parts, one for each index of `grp`. The reference program is written for one: setup_inputs(seed, part) draws one part's arguments, and reference() takes and returns one part's arrays. A program takes and returns all parts, laid end to end along the dimension named above; an argument that names none is the same for every part. Nothing has to cross between parts.
Inputs may be any that keep to these rules, and one draw needn't show every extreme that they name: The 32 samples of the k-th aligned block of sample_idx are distinct centres of the k-th block of 192 centres.
All inputs are finite; a program needn't handle non-finite values.
Results may differ from the reference program's by a relative error of at most 0.0031.
Values may be sent and summed in bfloat16 or wider, within the bound.
A program may use at most 128 MiB of HBM per device.

```python
import jax
import jax.numpy as jnp
from jax import lax

D = 768
CTR_DEV = 192
S_DEV = 32
NC = 3072
S = 512
N_CTR = 16


def draw_centres(key, part):
    first, second = jax.random.split(key)
    base = jax.random.normal(first, (NC, D), jnp.float32)
    scales = jnp.exp(jax.random.uniform(second, (NC, 1), jnp.float32, 0.0, 2.3))
    return (base * scales).astype(jnp.bfloat16)


def draw_sample_idx(key, part):
    blocks = S // S_DEV
    scores = jax.random.randint(key, (blocks, CTR_DEV), 0, 2 ** 20) * CTR_DEV + jnp.arange(CTR_DEV)[None, :]
    order = jnp.argsort(scores, axis=1, stable=True)[:, :S_DEV]
    base = (jnp.arange(blocks) * CTR_DEV)[:, None]
    return (order + base).reshape(S).astype(jnp.int32)


def draw_coef(key, part):
    values = jax.random.normal(key, (NC,), jnp.float32)
    return values * (4000.0 / jnp.sqrt(jnp.float32(NC)))


def gaussian(stream_key, extent, deviation, bound, kind=jnp.bfloat16):
    array = deviation * jax.random.normal(stream_key, extent, jnp.float32)
    return jnp.clip(array, min=-bound, max=bound).astype(kind)


def setup_inputs(seed: int = 0, part: int = 0) -> dict:
    seeds = jax.random.split(jax.random.key(seed), 5)
    part_splits = jax.random.split(jax.random.fold_in(seeds[4], part), 5)
    centres = draw_centres(jax.random.fold_in(jax.random.fold_in(seeds[4], part), 71), part)
    sample_idx = draw_sample_idx(jax.random.fold_in(jax.random.fold_in(seeds[4], part), 71), part)
    coef = draw_coef(jax.random.fold_in(jax.random.fold_in(seeds[4], part), 71), part)
    metric_factor = gaussian(seeds[3], (D, D), D ** -0.5, 0.21875)
    return {"centres": centres, "sample_idx": sample_idx, "coef": coef, "metric_factor": metric_factor}


def block_grad(u_all, su, v_blk, coef_blk):
    width = u_all.shape[1]
    sv = lax.optimization_barrier(jnp.sum(v_blk.astype(jnp.float32) ** 2, axis=1))
    cross = jnp.dot(u_all, v_blk.T, preferred_element_type=jnp.float32)
    dist_sq = jnp.maximum(su[:, None] + sv[None, :] - 2.0 * cross, 0.0)
    radius = jnp.sqrt(dist_sq / width + 1.0)
    weight = coef_blk[None, :] * jnp.exp(-radius / 4.0) / (4.0 * width * radius)
    wround = weight.astype(jnp.bfloat16)
    return jnp.dot(wround, v_blk, preferred_element_type=jnp.float32) - lax.optimization_barrier(jnp.sum(weight, axis=1))[:, None] * u_all.astype(jnp.float32)

def reference(centres, sample_idx, coef, metric_factor):
    samples = jnp.take(centres, sample_idx.astype(jnp.int32), axis=0)
    u_all = jnp.dot(samples, metric_factor, preferred_element_type=jnp.float32).astype(jnp.bfloat16)
    su = lax.optimization_barrier(jnp.sum(u_all.astype(jnp.float32) ** 2, axis=1))
    v_all = jnp.dot(centres, metric_factor, preferred_element_type=jnp.float32).astype(jnp.bfloat16)
    v_blocks = v_all.reshape(N_CTR, CTR_DEV, D)
    c_blocks = coef.reshape(N_CTR, CTR_DEV)

    def step(total, pair):
        return (total + block_grad(u_all, su, pair[0], pair[1]), None)
    start = jnp.zeros((u_all.shape[0], D), jnp.float32)
    grad_u, _ = lax.scan(step, start, (v_blocks, c_blocks))
    factor = metric_factor.astype(jnp.float32)
    grads = jnp.dot(grad_u, factor.T, precision=lax.Precision.HIGHEST)
    agop = jnp.dot(grads.T, grads, precision=lax.Precision.HIGHEST) / u_all.shape[0]
    metric_new = agop * D / jnp.trace(agop)
    transformed = jnp.dot(grads, metric_new, precision=lax.Precision.HIGHEST)
    return (metric_new, transformed)
```

```python
import functools

import jax
import jax.numpy as jnp
from jax import lax
from jax.experimental import pallas as pl
from jax.experimental.pallas import tpu as pltpu
from jax.sharding import PartitionSpec as P

F32 = jnp.float32
BF16 = jnp.bfloat16
NT = (((1,), (1,)), ((), ()))


def split(x):
    high = x.astype(BF16)
    return high, (x - high.astype(F32)).astype(BF16)


def kernel(
    A, B, c_ref, idx_ref, coef_ref, m_ref, metric_ref, out_ref,
    cent, cfs, ucol, vbuf, acc, psend, precv, gall,
    cs_send, cf_send, c_recv, cf_recv, u_send, u_recv, p_send, p_recv,
    gz_send, gy_send, gc_send, g_recv,
):
    own, width = c_ref.shape
    rows = idx_ref.shape[1]
    samples = A * B * 2 * rows
    me = lax.axis_index("ctr")
    c = lax.rem(me, 2)
    b = lax.rem(me // 2, B)
    a = me // (2 * B)

    def dev(a_, b_, c_):
        return {"ctr": (a_ * B + b_) * 2 + c_}

    def copy(src, dst, ssem, rsem, to):
        return pltpu.make_async_remote_copy(
            src_ref=src, dst_ref=dst, send_sem=ssem, recv_sem=rsem,
            device_id=to, device_id_type=pl.DeviceIdType.MESH,
        )

    partner = dev(a, b, 1 - c)
    barrier = pltpu.get_barrier_semaphore()
    peers = [dev(lax.rem(a + k, A), b, c) for k in range(1, A)]
    peers += [dev(a, lax.rem(b + k, B), c) for k in range(1, B)]
    peers += [partner]
    for peer in peers:
        pl.semaphore_signal(barrier, inc=1, device_id=peer, device_id_type=pl.DeviceIdType.MESH)
    pl.semaphore_wait(barrier, len(peers))

    slot = b * 2 + c
    sends = []
    for k in range(1, B):
        to = dev(a, lax.rem(b + k, B), c)
        sends.append(copy(c_ref, cent.at[slot], cs_send.at[k], c_recv.at[slot], to))
        sends.append(copy(coef_ref, cfs.at[slot], cf_send.at[k], cf_recv.at[slot], to))
    sends.append(copy(c_ref, cent.at[slot], cs_send.at[0], c_recv.at[slot], partner))
    sends.append(copy(coef_ref, cfs.at[slot], cf_send.at[0], cf_recv.at[slot], partner))
    for s in sends:
        s.start()

    diag = lax.broadcasted_iota(jnp.int32, (rows, rows), 0) == lax.broadcasted_iota(
        jnp.int32, (rows, rows), 1
    )
    local_idx = (idx_ref[...] - me * own).astype(F32)
    column = jnp.sum(
        jnp.where(diag, jnp.broadcast_to(local_idx, (rows, rows)), 0.0), axis=1, keepdims=True
    )
    places = lax.broadcasted_iota(jnp.int32, (rows, own), 1).astype(F32)
    pick = jnp.where(places == column, 1.0, 0.0).astype(BF16)
    picked = jnp.dot(pick, c_ref[...], preferred_element_type=F32).astype(BF16)
    ucol[a] = jnp.dot(picked, m_ref[...], preferred_element_type=F32).astype(BF16)
    for k in range(1, A):
        s = copy(
            ucol.at[a], ucol.at[a], u_send.at[k], u_recv.at[a], dev(lax.rem(a + k, A), b, c)
        )
        s.start()
        sends.append(s)

    def coords(block):
        vbuf[...] = jnp.dot(block, m_ref[...], preferred_element_type=F32).astype(BF16)

    def arrived(dst, rsem):
        copy(dst, dst, rsem, rsem, partner).wait_recv()

    coords(c_ref[...])
    for k in range(1, A):
        j = lax.rem(a + k, A)
        arrived(ucol.at[j], u_recv.at[j])
    acc[...] = jnp.zeros_like(acc)

    def add_block(coef_row):
        v = vbuf[...]
        u = ucol[...].reshape(A * rows, width)
        uf = u.astype(F32)
        su = jnp.sum(uf * uf, axis=1, keepdims=True)
        vf = v.astype(F32)
        high, low = split(vf * vf)
        ones = jnp.ones((16, width), BF16)
        sv = lax.dot_general(ones, high, NT, preferred_element_type=F32) + lax.dot_general(
            ones, low, NT, preferred_element_type=F32
        )
        cross = lax.dot_general(u, v, NT, preferred_element_type=F32)
        dist_sq = jnp.maximum(su + sv[0:1] - 2.0 * cross, 0.0)
        radius = jnp.sqrt(dist_sq / width + 1.0)
        weight = coef_row * jnp.exp(-radius / 4.0) / (4.0 * width * radius)
        acc[...] += (
            jnp.dot(weight.astype(BF16), v, preferred_element_type=F32)
            - jnp.sum(weight, axis=1, keepdims=True) * uf
        )

    def take(j):
        coords(cent[j])
        add_block(cfs[j])

    def wait_slot(j):
        arrived(cent.at[j], c_recv.at[j])
        arrived(cfs.at[j], cf_recv.at[j])

    add_block(coef_ref[...])
    other = b * 2 + 1 - c
    wait_slot(other)
    take(other)

    def forward(k, to_start):
        j = lax.rem(b + k, B) * 2 + c
        x = copy(cent.at[j], cent.at[j], cs_send.at[B - 1 + k], c_recv.at[j], partner)
        y = copy(cfs.at[j], cfs.at[j], cf_send.at[B - 1 + k], cf_recv.at[j], partner)
        if to_start:
            x.start()
            y.start()
        else:
            x.wait_send()
            y.wait_send()

    def row_step(k, _):
        same = lax.rem(b + k, B) * 2 + c
        wait_slot(same)
        forward(k, True)
        take(same)
        cross = lax.rem(b + k, B) * 2 + 1 - c
        wait_slot(cross)
        take(cross)
        forward(k, False)
        return 0

    lax.fori_loop(1, B, row_step, 0)

    psend[...] = acc[...].astype(BF16).reshape(A, rows, width)
    for k in range(1, A):
        j = lax.rem(a + k, A)
        s = copy(psend.at[j], precv.at[a], p_send.at[k], p_recv.at[a], dev(j, b, c))
        s.start()
        sends.append(s)
    total = acc[pl.ds(pl.multiple_of(a * rows, rows), rows), :]
    for k in range(1, A):
        j = lax.rem(a + k, A)
        arrived(precv.at[j], p_recv.at[j])
        total += precv[j].astype(F32)

    high, low = split(total)
    grads = lax.dot_general(high, m_ref[...], NT, preferred_element_type=F32) + lax.dot_general(
        low, m_ref[...], NT, preferred_element_type=F32
    )

    def place(a_, b_, c_):
        return (c_ * B + b_) * A + a_

    mine = place(a, b, c)
    gall[mine] = grads.astype(BF16)
    for k in range(1, A):
        s = copy(
            gall.at[mine], gall.at[mine], gz_send.at[k], g_recv.at[mine],
            dev(lax.rem(a + k, A), b, c),
        )
        s.start()
        sends.append(s)
    for k in range(A):
        j = place(lax.rem(a + k, A), b, c)
        if k:
            arrived(gall.at[j], g_recv.at[j])
        for q in range(1, B):
            s = copy(
                gall.at[j], gall.at[j], gy_send.at[k * B + q], g_recv.at[j],
                dev(a, lax.rem(b + q, B), c),
            )
            s.start()
            sends.append(s)
        s = copy(gall.at[j], gall.at[j], gc_send.at[k], g_recv.at[j], partner)
        s.start()
        sends.append(s)
    for k in range(A):
        for q in range(1, B):
            j = place(lax.rem(a + k, A), lax.rem(b + q, B), c)
            arrived(gall.at[j], g_recv.at[j])
            s = copy(gall.at[j], gall.at[j], gc_send.at[q * A + k], g_recv.at[j], partner)
            s.start()
            sends.append(s)
    for k in range(A):
        for q in range(B):
            j = place(lax.rem(a + k, A), lax.rem(b + q, B), 1 - c)
            arrived(gall.at[j], g_recv.at[j])

    metric_rows = metric_ref.shape[0]
    padded = -(-metric_rows // 16) * 16

    def squares(i, t):
        g = gall[i].astype(F32)
        return t + g * g

    square = lax.fori_loop(0, A * B * 2, squares, jnp.zeros((rows, width), F32))
    trace = jnp.sum(jnp.sum(square, axis=1, keepdims=True), axis=0, keepdims=True) / samples

    full = gall[...].reshape(samples, width)
    line = lax.broadcasted_iota(jnp.int32, (padded, width), 0) + me * metric_rows
    choose = jnp.where(
        line == lax.broadcasted_iota(jnp.int32, (padded, width), 1), 1.0, 0.0
    ).astype(BF16)
    ghigh, glow = split(grads)
    left = jnp.concatenate([choose, ghigh, glow], axis=0)
    inner = lax.dot_general(left, full, NT, preferred_element_type=F32)
    gram = inner[padded : padded + rows] + inner[padded + rows :]
    phigh, plow = split((gram / samples) * width / trace)
    left = jnp.concatenate([inner[:padded].astype(BF16), phigh, plow], axis=0)
    result = jnp.dot(left, full, preferred_element_type=F32)
    metric_ref[...] = (result[:metric_rows] / samples) * width / trace
    out_ref[...] = result[padded : padded + rows] + result[padded + rows :]

    for s in sends:
        s.wait_send()


def local(A, B, centres, sample_idx, coef, metric_factor):
    own, width = centres.shape
    rows = sample_idx.shape[0]
    n = A * B * 2
    dma = lambda k: pltpu.SemaphoreType.DMA((k,))
    vmem = pl.BlockSpec(memory_space=pltpu.VMEM)
    return pl.pallas_call(
        functools.partial(kernel, A, B),
        out_shape=(
            jax.ShapeDtypeStruct((width // n, width), F32),
            jax.ShapeDtypeStruct((rows, width), F32),
        ),
        in_specs=[vmem] * 4,
        out_specs=(vmem, vmem),
        scratch_shapes=[
            pltpu.VMEM((2 * B, own, width), BF16),
            pltpu.VMEM((2 * B, 1, own), F32),
            pltpu.VMEM((A, rows, width), BF16),
            pltpu.VMEM((own, width), BF16),
            pltpu.VMEM((A * rows, width), F32),
            pltpu.VMEM((A, rows, width), BF16),
            pltpu.VMEM((A, rows, width), BF16),
            pltpu.VMEM((n, rows, width), BF16),
            dma(2 * B), dma(2 * B), dma(2 * B), dma(2 * B),
            dma(A), dma(A), dma(A), dma(A),
            dma(A), dma(A * B), dma(A * B), dma(n),
        ],
        compiler_params=pltpu.CompilerParams(collective_id=0, has_side_effects=True),
    )(centres, sample_idx.reshape(1, rows), coef.reshape(1, own), metric_factor)


def solution(mesh):
    chips = mesh.shape["ctr"] // 2
    A = 1
    while A * A < chips:
        A *= 2
    B = chips // A
    placed = (P(("grp", "ctr"), None), P(("grp", "ctr")), P(("grp", "ctr")), P())
    return jax.shard_map(
        functools.partial(local, A, B),
        mesh=mesh,
        in_specs=placed,
        out_specs=(P(("grp", "ctr"), None), P(("grp", "ctr"), None)),
        check_vma=False,
    )
```

```python
import functools

import jax
import jax.numpy as jnp
from jax import lax
from jax.experimental import pallas as pl
from jax.experimental.pallas import tpu as pltpu
from jax.sharding import PartitionSpec as P

F32 = jnp.float32
BF16 = jnp.bfloat16
NT = (((1,), (1,)), ((), ()))


def parts(own):
    first = own // 256 * 128 + 128 if own > 128 else own
    return [(0, first)] + ([(first, own - first)] if first < own else [])


def split(x):
    high = x.astype(BF16)
    return high, (x - high.astype(F32)).astype(BF16)


def kernel(
    A, B, c_hbm, idx_hbm, coef_hbm, m_hbm, gall, grads_ref,
    c_ref, idx_ref, coef_ref, m_ref,
    cent, cfs, ucol, vbuf, acc, psend, precv,
    cs_send, cf_send, c_recv, cf_recv, u_send, u_recv, p_send, p_recv,
    gz_send, gy_send, gc_send, g_recv, load,
):
    own, width = c_ref.shape
    rows = idx_ref.shape[1]
    cuts = parts(own)
    H = len(cuts)
    me = lax.axis_index("ctr")
    c = lax.rem(me, 2)
    b = lax.rem(me // 2, B)
    a = me // (2 * B)

    def dev(a_, b_, c_):
        return {"ctr": (a_ * B + b_) * 2 + c_}

    def copy(src, dst, ssem, rsem, to):
        return pltpu.make_async_remote_copy(
            src_ref=src, dst_ref=dst, send_sem=ssem, recv_sem=rsem,
            device_id=to, device_id_type=pl.DeviceIdType.MESH,
        )

    partner = dev(a, b, 1 - c)
    barrier = pltpu.get_barrier_semaphore()
    peers = [dev(lax.rem(a + k, A), b, c) for k in range(1, A)]
    peers += [dev(a, lax.rem(b + k, B), c) for k in range(1, B)]
    peers += [partner]
    for peer in peers:
        pl.semaphore_signal(barrier, inc=1, device_id=peer, device_id_type=pl.DeviceIdType.MESH)
    loads = [
        pltpu.make_async_copy(src, dst, load.at[k])
        for k, (src, dst) in enumerate(
            [(idx_hbm, idx_ref), (c_hbm, c_ref), (m_hbm, m_ref), (coef_hbm, coef_ref)]
        )
    ]
    for item in loads:
        item.start()
    pl.semaphore_wait(barrier, len(peers))

    slot = b * 2 + c
    sends = []

    def piece(ref, h):
        return ref.at[pl.ds(cuts[h][0], cuts[h][1])]

    for k in range(1, B):
        to = dev(a, lax.rem(b + k, B), c)
        sends.append(copy(coef_hbm, cfs.at[slot], cf_send.at[k], cf_recv.at[slot], to))
    for h in range(H):
        for k in range(1, B):
            to = dev(a, lax.rem(b + k, B), c)
            sends.append(copy(
                piece(c_hbm, h), piece(cent.at[slot], h), cs_send.at[k * H + h],
                c_recv.at[slot * H + h], to,
            ))
    sends.append(copy(coef_hbm, cfs.at[slot], cf_send.at[0], cf_recv.at[slot], partner))
    for h in range(H):
        sends.append(copy(
            piece(c_hbm, h), piece(cent.at[slot], h), cs_send.at[h], c_recv.at[slot * H + h],
            partner,
        ))
    for s in sends:
        s.start()
    sign = 2 * (a // (A // 2)) - 1

    def along(k):
        return lax.rem(a + sign * k + A, A)

    diag = lax.broadcasted_iota(jnp.int32, (rows, rows), 0) == lax.broadcasted_iota(
        jnp.int32, (rows, rows), 1
    )
    loads[0].wait()
    loads[1].wait()
    local_idx = (idx_ref[...] - me * own).astype(F32)
    column = jnp.sum(
        jnp.where(diag, jnp.broadcast_to(local_idx, (rows, rows)), 0.0), axis=1, keepdims=True
    )
    places = lax.broadcasted_iota(jnp.int32, (rows, own), 1).astype(F32)
    pick = jnp.where(places == column, 1.0, 0.0).astype(BF16)
    picked = jnp.dot(pick, c_ref[...], preferred_element_type=F32).astype(BF16)
    loads[2].wait()
    ucol[a] = jnp.dot(picked, m_ref[...], preferred_element_type=F32).astype(BF16)
    for k in range(1, A):
        s = copy(
            ucol.at[a], ucol.at[a], u_send.at[k], u_recv.at[a], dev(along(k), b, c)
        )
        s.start()
        sends.append(s)

    def coords(block):
        vbuf[: block.shape[0]] = jnp.dot(
            block, m_ref[...], preferred_element_type=F32
        ).astype(BF16)

    def arrived(dst, rsem):
        copy(dst, dst, rsem, rsem, partner).wait_recv()

    coords(c_ref[...])
    for k in range(1, A):
        j = along(k)
        arrived(ucol.at[j], u_recv.at[j])
    acc[...] = jnp.zeros_like(acc)

    def add_block(coef_row):
        v = vbuf[: coef_row.shape[1]]
        u = ucol[...].reshape(A * rows, width)
        uf = u.astype(F32)
        su = jnp.sum(uf * uf, axis=1, keepdims=True)
        vf = v.astype(F32)
        high, low = split(vf * vf)
        ones = jnp.ones((16, width), BF16)
        sv = lax.dot_general(ones, high, NT, preferred_element_type=F32) + lax.dot_general(
            ones, low, NT, preferred_element_type=F32
        )
        cross = lax.dot_general(u, v, NT, preferred_element_type=F32)
        dist_sq = jnp.maximum(su + sv[0:1] - 2.0 * cross, 0.0)
        radius = jnp.sqrt(dist_sq / width + 1.0)
        weight = coef_row * jnp.exp(-radius / 4.0) / (4.0 * width * radius)
        acc[...] += (
            jnp.dot(weight.astype(BF16), v, preferred_element_type=F32)
            - jnp.sum(weight, axis=1, keepdims=True) * uf
        )

    def take(j, h):
        first, count = cuts[h]
        coords(cent[j, first : first + count])
        add_block(cfs[j][:, first : first + count])

    def wait_piece(j, h):
        x = piece(cent.at[j], h)
        arrived(x, c_recv.at[j * H + h])

    loads[3].wait()
    add_block(coef_ref[...])
    other = b * 2 + 1 - c
    arrived(cfs.at[other], cf_recv.at[other])
    for h in range(H):
        wait_piece(other, h)
    coords(cent[other])
    add_block(cfs[other])

    def row_step(k, _):
        same = lax.rem(b + k, B) * 2 + c
        cross = lax.rem(b + k, B) * 2 + 1 - c
        hops = []
        arrived(cfs.at[same], cf_recv.at[same])
        hops.append(copy(
            cfs.at[same], cfs.at[same], cf_send.at[B - 1 + k], cf_recv.at[same], partner
        ))
        hops[0].start()
        for h in range(H):
            wait_piece(same, h)
            hop = copy(
                piece(cent.at[same], h), piece(cent.at[same], h),
                cs_send.at[(B - 1 + k) * H + h], c_recv.at[same * H + h], partner,
            )
            hop.start()
            hops.append(hop)
            take(same, h)
            if h == 0:
                arrived(cfs.at[cross], cf_recv.at[cross])
            wait_piece(cross, h)
            take(cross, h)
        for hop in hops:
            hop.wait_send()
        return 0

    lax.fori_loop(1, B, row_step, 0)

    psend[...] = acc[...].astype(BF16).reshape(A, rows, width)
    for k in range(1, A):
        j = along(k)
        s = copy(psend.at[j], precv.at[a], p_send.at[k], p_recv.at[a], dev(j, b, c))
        s.start()
        sends.append(s)
    total = acc[pl.ds(pl.multiple_of(a * rows, rows), rows), :]
    for k in range(1, A):
        j = along(k)
        arrived(precv.at[j], p_recv.at[j])
        total += precv[j].astype(F32)

    high, low = split(total)
    grads = lax.dot_general(high, m_ref[...], NT, preferred_element_type=F32) + lax.dot_general(
        low, m_ref[...], NT, preferred_element_type=F32
    )

    def place(a_, b_, c_):
        return (c_ * B + b_) * A + a_

    mine = place(a, b, c)
    gall[mine] = grads.astype(BF16)
    grads_ref[...] = grads
    for k in range(1, A):
        s = copy(
            gall.at[mine], gall.at[mine], gz_send.at[k], g_recv.at[mine],
            dev(along(k), b, c),
        )
        s.start()
        sends.append(s)
    for k in range(A):
        j = place(along(k), b, c)
        if k:
            arrived(gall.at[j], g_recv.at[j])
        for q in range(1, B):
            s = copy(
                gall.at[j], gall.at[j], gy_send.at[k * B + q], g_recv.at[j],
                dev(a, lax.rem(b + q, B), c),
            )
            s.start()
            sends.append(s)
        s = copy(gall.at[j], gall.at[j], gc_send.at[k], g_recv.at[j], partner)
        s.start()
        sends.append(s)
    for k in range(A):
        for q in range(1, B):
            j = place(along(k), lax.rem(b + q, B), c)
            arrived(gall.at[j], g_recv.at[j])
            s = copy(gall.at[j], gall.at[j], gc_send.at[q * A + k], g_recv.at[j], partner)
            s.start()
            sends.append(s)
    for k in range(A):
        for q in range(B):
            j = place(lax.rem(a + k, A), lax.rem(b + q, B), 1 - c)
            arrived(gall.at[j], g_recv.at[j])

    for s in sends:
        s.wait_send()


def finish(gall, grads_ref, metric_ref, out_ref):
    blocks, rows, width = gall.shape
    samples = blocks * rows
    me = lax.axis_index("ctr")
    grads = grads_ref[...]
    metric_rows = metric_ref.shape[0]
    padded = -(-metric_rows // 16) * 16

    def squares(i, t):
        g = gall[i].astype(F32)
        return t + g * g

    square = lax.fori_loop(0, blocks, squares, jnp.zeros((rows, width), F32))
    trace = jnp.sum(jnp.sum(square, axis=1, keepdims=True), axis=0, keepdims=True) / samples

    full = gall[...].reshape(samples, width)
    line = lax.broadcasted_iota(jnp.int32, (padded, width), 0) + me * metric_rows
    choose = jnp.where(
        line == lax.broadcasted_iota(jnp.int32, (padded, width), 1), 1.0, 0.0
    ).astype(BF16)
    ghigh, glow = split(grads)
    left = jnp.concatenate([choose, ghigh, glow], axis=0)
    inner = lax.dot_general(left, full, NT, preferred_element_type=F32)
    gram = inner[padded : padded + rows] + inner[padded + rows :]
    phigh, plow = split((gram / samples) * width / trace)
    left = jnp.concatenate([inner[:padded].astype(BF16), phigh, plow], axis=0)
    result = jnp.dot(left, full, preferred_element_type=F32)
    metric_ref[...] = (result[:metric_rows] / samples) * width / trace
    out_ref[...] = result[padded : padded + rows] + result[padded + rows :]


def local(A, B, centres, sample_idx, coef, metric_factor):
    own, width = centres.shape
    rows = sample_idx.shape[0]
    n = A * B * 2
    dma = lambda k: pltpu.SemaphoreType.DMA((k,))
    vmem = pl.BlockSpec(memory_space=pltpu.VMEM)
    H = len(parts(own))
    limit = 67043328 - (n * 2 + 4) * rows * width
    hbm = pl.BlockSpec(memory_space=pltpu.HBM)
    gall, grads = pl.pallas_call(
        functools.partial(kernel, A, B),
        out_shape=(pltpu.VMEM((n, rows, width), BF16), pltpu.VMEM((rows, width), F32)),
        in_specs=[hbm] * 4,
        out_specs=(vmem, vmem),
        scratch_shapes=[
            pltpu.VMEM((own, width), BF16),
            pltpu.VMEM((1, rows), jnp.int32),
            pltpu.VMEM((1, own), F32),
            pltpu.VMEM((width, width), BF16),
            pltpu.VMEM((2 * B, own, width), BF16),
            pltpu.VMEM((2 * B, 1, own), F32),
            pltpu.VMEM((A, rows, width), BF16),
            pltpu.VMEM((own, width), BF16),
            pltpu.VMEM((A * rows, width), F32),
            pltpu.VMEM((A, rows, width), BF16),
            pltpu.VMEM((A, rows, width), BF16),
            dma(2 * B * H), dma(2 * B), dma(2 * B * H), dma(2 * B),
            dma(A), dma(A), dma(A), dma(A),
            dma(A), dma(A * B), dma(A * B), dma(n), dma(4),
        ],
        compiler_params=pltpu.CompilerParams(
            collective_id=0, has_side_effects=True, vmem_limit_bytes=limit
        ),
    )(centres, sample_idx.reshape(1, rows), coef.reshape(1, own), metric_factor)
    return pl.pallas_call(
        finish,
        out_shape=(
            jax.ShapeDtypeStruct((width // n, width), F32),
            jax.ShapeDtypeStruct((rows, width), F32),
        ),
        in_specs=[vmem] * 2,
        out_specs=(vmem, vmem),
        compiler_params=pltpu.CompilerParams(vmem_limit_bytes=40 * 2**20),
    )(gall, grads)


def solution(mesh):
    chips = mesh.shape["ctr"] // 2
    A = 1
    while A * A < chips:
        A *= 2
    B = chips // A
    placed = (P(("grp", "ctr"), None), P(("grp", "ctr")), P(("grp", "ctr")), P())
    return jax.shard_map(
        functools.partial(local, A, B),
        mesh=mesh,
        in_specs=placed,
        out_specs=(P(("grp", "ctr"), None), P(("grp", "ctr"), None)),
        check_vma=False,
    )
```

```python
import functools

import jax
import jax.numpy as jnp
from jax import lax
from jax.experimental import pallas as pl
from jax.experimental.pallas import tpu as pltpu
from jax.sharding import PartitionSpec as P

F32 = jnp.float32
BF16 = jnp.bfloat16
NT = (((1,), (1,)), ((), ()))


def parts(own):
    first = own
    return [(0, first)] + ([(first, own - first)] if first < own else [])


def split(x):
    high = x.astype(BF16)
    return high, (x - high.astype(F32)).astype(BF16)


def kernel(
    A, B, c_hbm, idx_hbm, coef_hbm, m_hbm, gall, grads_ref,
    c_ref, idx_ref, coef_ref, m_ref,
    cent, cfs, ucol, vbuf, acc, su_ref, wsum, psend, precv,
    cs_send, cf_send, c_recv, cf_recv, u_send, u_recv, p_send, p_recv,
    gz_send, gy_send, gc_send, g_recv, load,
):
    own, width = c_ref.shape
    rows = idx_ref.shape[1]
    cuts = parts(own)
    H = len(cuts)
    me = lax.axis_index("ctr")
    c = lax.rem(me, 2)
    b = lax.rem(me // 2, B)
    a = me // (2 * B)

    def dev(a_, b_, c_):
        return {"ctr": (a_ * B + b_) * 2 + c_}

    def copy(src, dst, ssem, rsem, to):
        return pltpu.make_async_remote_copy(
            src_ref=src, dst_ref=dst, send_sem=ssem, recv_sem=rsem,
            device_id=to, device_id_type=pl.DeviceIdType.MESH,
        )

    partner = dev(a, b, 1 - c)
    barrier = pltpu.get_barrier_semaphore()
    peers = [dev(lax.rem(a + k, A), b, c) for k in range(1, A)]
    peers += [dev(a, lax.rem(b + k, B), c) for k in range(1, B)]
    peers += [partner]
    for peer in peers:
        pl.semaphore_signal(barrier, inc=1, device_id=peer, device_id_type=pl.DeviceIdType.MESH)
    loads = [
        pltpu.make_async_copy(src, dst, load.at[k])
        for k, (src, dst) in enumerate(
            [(idx_hbm, idx_ref), (c_hbm, c_ref), (m_hbm, m_ref), (coef_hbm, coef_ref)]
        )
    ]
    for item in loads:
        item.start()
    pl.semaphore_wait(barrier, len(peers))

    slot = b * 2 + c
    sends = []

    def piece(ref, h):
        return ref.at[pl.ds(cuts[h][0], cuts[h][1])]

    for k in range(1, B):
        to = dev(a, lax.rem(b + k, B), c)
        sends.append(copy(coef_hbm, cfs.at[slot], cf_send.at[k], cf_recv.at[slot], to))
    for h in range(H):
        for k in range(1, B):
            to = dev(a, lax.rem(b + k, B), c)
            sends.append(copy(
                piece(c_hbm, h), piece(cent.at[slot], h), cs_send.at[k * H + h],
                c_recv.at[slot * H + h], to,
            ))
    sends.append(copy(coef_hbm, cfs.at[slot], cf_send.at[0], cf_recv.at[slot], partner))
    for h in range(H):
        sends.append(copy(
            piece(c_hbm, h), piece(cent.at[slot], h), cs_send.at[h], c_recv.at[slot * H + h],
            partner,
        ))
    for s in sends:
        s.start()
    sign = 2 * (a // (A // 2)) - 1

    def along(k):
        return lax.rem(a + sign * k + A, A)

    diag = lax.broadcasted_iota(jnp.int32, (rows, rows), 0) == lax.broadcasted_iota(
        jnp.int32, (rows, rows), 1
    )
    loads[0].wait()
    loads[1].wait()
    local_idx = (idx_ref[...] - me * own).astype(F32)
    column = jnp.sum(
        jnp.where(diag, jnp.broadcast_to(local_idx, (rows, rows)), 0.0), axis=1, keepdims=True
    )
    places = lax.broadcasted_iota(jnp.int32, (rows, own), 1).astype(F32)
    pick = jnp.where(places == column, 1.0, 0.0).astype(BF16)
    picked = jnp.dot(pick, c_ref[...], preferred_element_type=F32).astype(BF16)
    loads[2].wait()
    ucol[a] = jnp.dot(picked, m_ref[...], preferred_element_type=F32).astype(BF16)
    for k in range(1, A):
        s = copy(
            ucol.at[a], ucol.at[a], u_send.at[k], u_recv.at[a], dev(along(k), b, c)
        )
        s.start()
        sends.append(s)

    def coords(block):
        return jnp.dot(block, m_ref[...], preferred_element_type=F32).astype(BF16)

    def arrived(dst, rsem):
        copy(dst, dst, rsem, rsem, partner).wait_recv()

    def wait_piece(j, h):
        arrived(piece(cent.at[j], h), c_recv.at[j * H + h])

    def relay(k, h):
        j = lax.rem(b + k, B) * 2 + c
        wait_piece(j, h)
        first, count = cuts[h]
        cent[j, first : first + count] = coords(cent[j, first : first + count])
        hop = copy(
            piece(cent.at[j], h), piece(cent.at[j], h),
            cs_send.at[(B - 1 + k) * H + h], c_recv.at[j * H + h], partner,
        )
        hop.start()
        hops = [hop]
        if h == 0:
            arrived(cfs.at[j], cf_recv.at[j])
            hop = copy(cfs.at[j], cfs.at[j], cf_send.at[B - 1 + k], cf_recv.at[j], partner)
            hop.start()
            hops.append(hop)
        return hops

    vbuf[...] = coords(c_ref[...])
    other = b * 2 + 1 - c
    for h in range(H):
        wait_piece(other, h)
    cent[other] = coords(cent[other])
    early = relay(1, 0)
    for k in range(1, A):
        j = along(k)
        arrived(ucol.at[j], u_recv.at[j])
    uf = ucol[...].reshape(A * rows, width).astype(F32)
    su_ref[...] = jnp.sum(uf * uf, axis=1, keepdims=True)
    acc[...] = jnp.zeros_like(acc)
    wsum[...] = jnp.zeros_like(wsum)

    def add_block(v, coef_row):
        u = ucol[...].reshape(A * rows, width)
        vf = v.astype(F32)
        high, low = split(vf * vf)
        ones = jnp.ones((16, width), BF16)
        sv = lax.dot_general(ones, high, NT, preferred_element_type=F32) + lax.dot_general(
            ones, low, NT, preferred_element_type=F32
        )
        cross = lax.dot_general(u, v, NT, preferred_element_type=F32)
        dist_sq = jnp.maximum(su_ref[...] + sv[0:1] - 2.0 * cross, 0.0)
        radius = jnp.sqrt(dist_sq / width + 1.0)
        weight = coef_row * jnp.exp(-radius / 4.0) / (4.0 * width * radius)
        acc[...] += jnp.dot(weight.astype(BF16), v, preferred_element_type=F32)
        wsum[...] += jnp.sum(weight, axis=1, keepdims=True)

    loads[3].wait()
    add_block(vbuf[...], coef_ref[...])
    arrived(cfs.at[other], cf_recv.at[other])
    add_block(cent[other], cfs[other])

    def row_step(k, hops):
        same = lax.rem(b + k, B) * 2 + c
        cross = lax.rem(b + k, B) * 2 + 1 - c
        for h in range(1, H):
            hops = hops + relay(k, h)
        add_block(cent[same], cfs[same])
        arrived(cfs.at[cross], cf_recv.at[cross])
        for h in range(H):
            wait_piece(cross, h)
        add_block(cent[cross], cfs[cross])
        return hops

    sends += row_step(1, early)

    def later_step(k, _):
        for hop in row_step(k, relay(k, 0)):
            hop.wait_send()
        return 0

    if B > 2:
        lax.fori_loop(2, B, later_step, 0)
    acc[...] -= wsum[...] * ucol[...].reshape(A * rows, width).astype(F32)

    psend[...] = acc[...].astype(BF16).reshape(A, rows, width)
    for k in range(1, A):
        j = lax.rem(a + k, A)
        s = copy(psend.at[j], precv.at[a], p_send.at[k], p_recv.at[a], dev(j, b, c))
        s.start()
        sends.append(s)
    total = acc[pl.ds(pl.multiple_of(a * rows, rows), rows), :]
    for k in range(1, A):
        j = along(k)
        arrived(precv.at[j], p_recv.at[j])
        total += precv[j].astype(F32)

    high, low = split(total)
    grads = lax.dot_general(high, m_ref[...], NT, preferred_element_type=F32) + lax.dot_general(
        low, m_ref[...], NT, preferred_element_type=F32
    )

    def place(a_, b_, c_):
        return (c_ * B + b_) * A + a_

    mine = place(a, b, c)
    gall[mine] = grads.astype(BF16)
    grads_ref[...] = grads
    for k in range(1, A):
        s = copy(
            gall.at[mine], gall.at[mine], gz_send.at[k], g_recv.at[mine],
            dev(along(k), b, c),
        )
        s.start()
        sends.append(s)
    for k in range(A):
        j = place(along(k), b, c)
        if k:
            arrived(gall.at[j], g_recv.at[j])
        for q in range(1, B):
            s = copy(
                gall.at[j], gall.at[j], gy_send.at[k * B + q], g_recv.at[j],
                dev(a, lax.rem(b + q, B), c),
            )
            s.start()
            sends.append(s)
        s = copy(gall.at[j], gall.at[j], gc_send.at[k], g_recv.at[j], partner)
        s.start()
        sends.append(s)
    for k in range(A):
        for q in range(1, B):
            j = place(along(k), lax.rem(b + q, B), c)
            arrived(gall.at[j], g_recv.at[j])
            s = copy(gall.at[j], gall.at[j], gc_send.at[q * A + k], g_recv.at[j], partner)
            s.start()
            sends.append(s)
    for k in range(A):
        for q in range(B):
            j = place(lax.rem(a + k, A), lax.rem(b + q, B), 1 - c)
            arrived(gall.at[j], g_recv.at[j])

    for s in sends:
        s.wait_send()


def finish(gall, grads_ref, metric_ref, out_ref):
    blocks, rows, width = gall.shape
    samples = blocks * rows
    me = lax.axis_index("ctr")
    grads = grads_ref[...]
    metric_rows = metric_ref.shape[0]
    padded = -(-metric_rows // 16) * 16

    def squares(i, t):
        g = gall[i].astype(F32)
        return t + g * g

    square = lax.fori_loop(0, blocks, squares, jnp.zeros((rows, width), F32))
    trace = jnp.sum(jnp.sum(square, axis=1, keepdims=True), axis=0, keepdims=True) / samples

    full = gall[...].reshape(samples, width)
    line = lax.broadcasted_iota(jnp.int32, (padded, width), 0) + me * metric_rows
    choose = jnp.where(
        line == lax.broadcasted_iota(jnp.int32, (padded, width), 1), 1.0, 0.0
    ).astype(BF16)
    ghigh, glow = split(grads)
    left = jnp.concatenate([choose, ghigh, glow], axis=0)
    inner = lax.dot_general(left, full, NT, preferred_element_type=F32)
    gram = inner[padded : padded + rows] + inner[padded + rows :]
    phigh, plow = split((gram / samples) * width / trace)
    left = jnp.concatenate([inner[:padded].astype(BF16), phigh, plow], axis=0)
    result = jnp.dot(left, full, preferred_element_type=F32)
    metric_ref[...] = (result[:metric_rows] / samples) * width / trace
    out_ref[...] = result[padded : padded + rows] + result[padded + rows :]


def local(A, B, centres, sample_idx, coef, metric_factor):
    own, width = centres.shape
    rows = sample_idx.shape[0]
    n = A * B * 2
    dma = lambda k: pltpu.SemaphoreType.DMA((k,))
    vmem = pl.BlockSpec(memory_space=pltpu.VMEM)
    H = len(parts(own))
    limit = 67043328 - (n * 2 + 4) * rows * width
    hbm = pl.BlockSpec(memory_space=pltpu.HBM)
    gall, grads = pl.pallas_call(
        functools.partial(kernel, A, B),
        out_shape=(pltpu.VMEM((n, rows, width), BF16), pltpu.VMEM((rows, width), F32)),
        in_specs=[hbm] * 4,
        out_specs=(vmem, vmem),
        scratch_shapes=[
            pltpu.VMEM((own, width), BF16),
            pltpu.VMEM((1, rows), jnp.int32),
            pltpu.VMEM((1, own), F32),
            pltpu.VMEM((width, width), BF16),
            pltpu.VMEM((2 * B, own, width), BF16),
            pltpu.VMEM((2 * B, 1, own), F32),
            pltpu.VMEM((A, rows, width), BF16),
            pltpu.VMEM((own, width), BF16),
            pltpu.VMEM((A * rows, width), F32),
            pltpu.VMEM((A * rows, 1), F32),
            pltpu.VMEM((A * rows, 1), F32),
            pltpu.VMEM((A, rows, width), BF16),
            pltpu.VMEM((A, rows, width), BF16),
            dma(2 * B * H), dma(2 * B), dma(2 * B * H), dma(2 * B),
            dma(A), dma(A), dma(A), dma(A),
            dma(A), dma(A * B), dma(A * B), dma(n), dma(4),
        ],
        compiler_params=pltpu.CompilerParams(
            collective_id=0, has_side_effects=True, vmem_limit_bytes=limit
        ),
    )(centres, sample_idx.reshape(1, rows), coef.reshape(1, own), metric_factor)
    return pl.pallas_call(
        finish,
        out_shape=(
            jax.ShapeDtypeStruct((width // n, width), F32),
            jax.ShapeDtypeStruct((rows, width), F32),
        ),
        in_specs=[vmem] * 2,
        out_specs=(vmem, vmem),
        compiler_params=pltpu.CompilerParams(vmem_limit_bytes=40 * 2**20),
    )(gall, grads)


def solution(mesh):
    chips = mesh.shape["ctr"] // 2
    A = 1
    while A * A < chips:
        A *= 2
    B = chips // A
    placed = (P(("grp", "ctr"), None), P(("grp", "ctr")), P(("grp", "ctr")), P())
    return jax.shard_map(
        functools.partial(local, A, B),
        mesh=mesh,
        in_specs=placed,
        out_specs=(P(("grp", "ctr"), None), P(("grp", "ctr"), None)),
        check_vma=False,
    )
```

```python
import functools

import jax
import jax.numpy as jnp
from jax import lax
from jax.experimental import pallas as pl
from jax.experimental.pallas import tpu as pltpu
from jax.sharding import PartitionSpec as P

F32 = jnp.float32
BF16 = jnp.bfloat16
NT = (((1,), (1,)), ((), ()))


def parts(own):
    first = own
    return [(0, first)] + ([(first, own - first)] if first < own else [])


def split(x):
    high = x.astype(BF16)
    return high, (x - high.astype(F32)).astype(BF16)


def kernel(
    A, B, c_hbm, idx_hbm, coef_hbm, m_hbm, gall, grads_ref,
    c_ref, idx_ref, coef_ref, m_ref,
    cent, cfs, ucol, vbuf, acc, su_ref, wsum, psend, precv,
    cs_send, cf_send, c_recv, cf_recv, u_send, u_recv, p_send, p_recv,
    gz_send, gy_send, gc_send, g_recv, load,
):
    own, width = c_ref.shape
    rows = idx_ref.shape[1]
    cuts = parts(own)
    H = len(cuts)
    me = lax.axis_index("ctr")
    c = lax.rem(me, 2)
    b = lax.rem(me // 2, B)
    a = me // (2 * B)

    def dev(a_, b_, c_):
        return {"ctr": (a_ * B + b_) * 2 + c_}

    def copy(src, dst, ssem, rsem, to):
        return pltpu.make_async_remote_copy(
            src_ref=src, dst_ref=dst, send_sem=ssem, recv_sem=rsem,
            device_id=to, device_id_type=pl.DeviceIdType.MESH,
        )

    partner = dev(a, b, 1 - c)
    barrier = pltpu.get_barrier_semaphore()
    peers = [dev(lax.rem(a + k, A), b, c) for k in range(1, A)]
    peers += [dev(a, lax.rem(b + k, B), c) for k in range(1, B)]
    peers += [partner]
    for peer in peers:
        pl.semaphore_signal(barrier, inc=1, device_id=peer, device_id_type=pl.DeviceIdType.MESH)
    loads = [
        pltpu.make_async_copy(src, dst, load.at[k])
        for k, (src, dst) in enumerate(
            [(idx_hbm, idx_ref), (c_hbm, c_ref), (m_hbm, m_ref), (coef_hbm, coef_ref)]
        )
    ]
    for item in loads:
        item.start()
    pl.semaphore_wait(barrier, len(peers))

    slot = b * 2 + c
    sends = []

    def piece(ref, h):
        return ref.at[pl.ds(cuts[h][0], cuts[h][1])]

    for k in range(1, B):
        to = dev(a, lax.rem(b + k, B), c)
        sends.append(copy(coef_hbm, cfs.at[slot], cf_send.at[k], cf_recv.at[slot], to))
    for h in range(H):
        for k in range(1, B):
            to = dev(a, lax.rem(b + k, B), c)
            sends.append(copy(
                piece(c_hbm, h), piece(cent.at[slot], h), cs_send.at[k * H + h],
                c_recv.at[slot * H + h], to,
            ))
    sends.append(copy(coef_hbm, cfs.at[slot], cf_send.at[0], cf_recv.at[slot], partner))
    for h in range(H):
        sends.append(copy(
            piece(c_hbm, h), piece(cent.at[slot], h), cs_send.at[h], c_recv.at[slot * H + h],
            partner,
        ))
    for s in sends:
        s.start()
    sign = 2 * (a // (A // 2)) - 1

    def along(k):
        return lax.rem(a + sign * k + A, A)

    diag = lax.broadcasted_iota(jnp.int32, (rows, rows), 0) == lax.broadcasted_iota(
        jnp.int32, (rows, rows), 1
    )
    loads[0].wait()
    loads[1].wait()
    local_idx = (idx_ref[...] - me * own).astype(F32)
    column = jnp.sum(
        jnp.where(diag, jnp.broadcast_to(local_idx, (rows, rows)), 0.0), axis=1, keepdims=True
    )
    places = lax.broadcasted_iota(jnp.int32, (rows, own), 1).astype(F32)
    pick = jnp.where(places == column, 1.0, 0.0).astype(BF16)
    picked = jnp.dot(pick, c_ref[...], preferred_element_type=F32).astype(BF16)
    loads[2].wait()
    ucol[a] = jnp.dot(picked, m_ref[...], preferred_element_type=F32).astype(BF16)
    for k in range(1, A):
        s = copy(
            ucol.at[a], ucol.at[a], u_send.at[k], u_recv.at[a], dev(along(k), b, c)
        )
        s.start()
        sends.append(s)

    def coords(block):
        return jnp.dot(block, m_ref[...], preferred_element_type=F32).astype(BF16)

    def arrived(dst, rsem):
        copy(dst, dst, rsem, rsem, partner).wait_recv()

    def wait_piece(j, h):
        arrived(piece(cent.at[j], h), c_recv.at[j * H + h])

    def relay(k, h):
        j = lax.rem(b + k, B) * 2 + c
        wait_piece(j, h)
        first, count = cuts[h]
        cent[j, first : first + count] = coords(cent[j, first : first + count])
        hop = copy(
            piece(cent.at[j], h), piece(cent.at[j], h),
            cs_send.at[(B - 1 + k) * H + h], c_recv.at[j * H + h], partner,
        )
        hop.start()
        hops = [hop]
        if h == 0:
            arrived(cfs.at[j], cf_recv.at[j])
            hop = copy(cfs.at[j], cfs.at[j], cf_send.at[B - 1 + k], cf_recv.at[j], partner)
            hop.start()
            hops.append(hop)
        return hops

    vbuf[...] = coords(c_ref[...])
    other = b * 2 + 1 - c
    for h in range(H):
        wait_piece(other, h)
    cent[other] = coords(cent[other])
    early = relay(1, 0)
    for k in range(1, A):
        j = along(k)
        arrived(ucol.at[j], u_recv.at[j])
    uf = ucol[...].reshape(A * rows, width).astype(F32)
    su_ref[...] = jnp.sum(uf * uf, axis=1, keepdims=True)
    acc[...] = jnp.zeros_like(acc)
    wsum[...] = jnp.zeros_like(wsum)

    def add_block(v, coef_row):
        u = ucol[...].reshape(A * rows, width)
        vf = v.astype(F32)
        high, low = split(vf * vf)
        ones = jnp.ones((16, width), BF16)
        sv = lax.dot_general(ones, high, NT, preferred_element_type=F32) + lax.dot_general(
            ones, low, NT, preferred_element_type=F32
        )
        cross = lax.dot_general(u, v, NT, preferred_element_type=F32)
        dist_sq = jnp.maximum(su_ref[...] + sv[0:1] - 2.0 * cross, 0.0)
        radius = jnp.sqrt(dist_sq / width + 1.0)
        weight = coef_row * jnp.exp(-radius / 4.0) / (4.0 * width * radius)
        acc[...] += jnp.dot(weight.astype(BF16), v, preferred_element_type=F32)
        wsum[...] += jnp.sum(weight, axis=1, keepdims=True)

    loads[3].wait()
    add_block(vbuf[...], coef_ref[...])
    arrived(cfs.at[other], cf_recv.at[other])
    add_block(cent[other], cfs[other])

    def row_step(k, hops):
        same = lax.rem(b + k, B) * 2 + c
        cross = lax.rem(b + k, B) * 2 + 1 - c
        for h in range(1, H):
            hops = hops + relay(k, h)
        add_block(cent[same], cfs[same])
        arrived(cfs.at[cross], cf_recv.at[cross])
        for h in range(H):
            wait_piece(cross, h)
        add_block(cent[cross], cfs[cross])
        return hops

    sends += row_step(1, early)

    def later_step(k, _):
        for hop in row_step(k, relay(k, 0)):
            hop.wait_send()
        return 0

    if B > 2:
        lax.fori_loop(2, B, later_step, 0)
    acc[...] -= wsum[...] * ucol[...].reshape(A * rows, width).astype(F32)

    psend[...] = acc[...].astype(BF16).reshape(A, rows, width)
    for k in range(1, A):
        j = lax.rem(a + k, A)
        s = copy(psend.at[j], precv.at[a], p_send.at[k], p_recv.at[a], dev(j, b, c))
        s.start()
        sends.append(s)
    total = acc[pl.ds(pl.multiple_of(a * rows, rows), rows), :]
    for k in range(1, A):
        j = along(k)
        arrived(precv.at[j], p_recv.at[j])
        total += precv[j].astype(F32)

    high, low = split(total)
    both = lax.dot_general(
        jnp.concatenate([high, low], axis=0), m_ref[...], NT, preferred_element_type=F32
    )
    grads = both[:rows] + both[rows:]

    def place(a_, b_, c_):
        return (c_ * B + b_) * A + a_

    mine = place(a, b, c)
    gall[mine] = grads.astype(BF16)
    grads_ref[...] = grads
    for k in range(1, A):
        s = copy(
            gall.at[mine], gall.at[mine], gz_send.at[k], g_recv.at[mine],
            dev(along(k), b, c),
        )
        s.start()
        sends.append(s)
    for k in range(A):
        j = place(along(k), b, c)
        if k:
            arrived(gall.at[j], g_recv.at[j])
        for q in range(1, B):
            s = copy(
                gall.at[j], gall.at[j], gy_send.at[k * B + q], g_recv.at[j],
                dev(a, lax.rem(b + q, B), c),
            )
            s.start()
            sends.append(s)
        s = copy(gall.at[j], gall.at[j], gc_send.at[k], g_recv.at[j], partner)
        s.start()
        sends.append(s)
    for k in range(A):
        for q in range(1, B):
            j = place(along(k), lax.rem(b + q, B), c)
            arrived(gall.at[j], g_recv.at[j])
            s = copy(gall.at[j], gall.at[j], gc_send.at[q * A + k], g_recv.at[j], partner)
            s.start()
            sends.append(s)
    for k in range(A):
        for q in range(B):
            j = place(lax.rem(a + k, A), lax.rem(b + q, B), 1 - c)
            arrived(gall.at[j], g_recv.at[j])

    for s in sends:
        s.wait_send()


def finish(gall, grads_ref, metric_ref, out_ref):
    blocks, rows, width = gall.shape
    samples = blocks * rows
    me = lax.axis_index("ctr")
    grads = grads_ref[...]
    metric_rows = metric_ref.shape[0]
    padded = -(-metric_rows // 16) * 16

    def squares(i, t):
        g = gall[i].astype(F32)
        return t + g * g

    square = lax.fori_loop(0, blocks, squares, jnp.zeros((rows, width), F32))
    trace = jnp.sum(jnp.sum(square, axis=1, keepdims=True), axis=0, keepdims=True) / samples

    full = gall[...].reshape(samples, width)
    line = lax.broadcasted_iota(jnp.int32, (padded, width), 0) + me * metric_rows
    choose = jnp.where(
        line == lax.broadcasted_iota(jnp.int32, (padded, width), 1), 1.0, 0.0
    ).astype(BF16)
    ghigh, glow = split(grads)
    left = jnp.concatenate([choose, ghigh, glow], axis=0)
    inner = lax.dot_general(left, full, NT, preferred_element_type=F32)
    gram = inner[padded : padded + rows] + inner[padded + rows :]
    phigh, plow = split((gram / samples) * width / trace)
    left = jnp.concatenate([inner[:padded].astype(BF16), phigh, plow], axis=0)
    result = jnp.dot(left, full, preferred_element_type=F32)
    metric_ref[...] = (result[:metric_rows] / samples) * width / trace
    out_ref[...] = result[padded : padded + rows] + result[padded + rows :]


def local(A, B, centres, sample_idx, coef, metric_factor):
    own, width = centres.shape
    rows = sample_idx.shape[0]
    n = A * B * 2
    dma = lambda k: pltpu.SemaphoreType.DMA((k,))
    vmem = pl.BlockSpec(memory_space=pltpu.VMEM)
    H = len(parts(own))
    limit = 67043328 - (n * 2 + 4) * rows * width
    hbm = pl.BlockSpec(memory_space=pltpu.HBM)
    gall, grads = pl.pallas_call(
        functools.partial(kernel, A, B),
        out_shape=(pltpu.VMEM((n, rows, width), BF16), pltpu.VMEM((rows, width), F32)),
        in_specs=[hbm] * 4,
        out_specs=(vmem, vmem),
        scratch_shapes=[
            pltpu.VMEM((own, width), BF16),
            pltpu.VMEM((1, rows), jnp.int32),
            pltpu.VMEM((1, own), F32),
            pltpu.VMEM((width, width), BF16),
            pltpu.VMEM((2 * B, own, width), BF16),
            pltpu.VMEM((2 * B, 1, own), F32),
            pltpu.VMEM((A, rows, width), BF16),
            pltpu.VMEM((own, width), BF16),
            pltpu.VMEM((A * rows, width), F32),
            pltpu.VMEM((A * rows, 1), F32),
            pltpu.VMEM((A * rows, 1), F32),
            pltpu.VMEM((A, rows, width), BF16),
            pltpu.VMEM((A, rows, width), BF16),
            dma(2 * B * H), dma(2 * B), dma(2 * B * H), dma(2 * B),
            dma(A), dma(A), dma(A), dma(A),
            dma(A), dma(A * B), dma(A * B), dma(n), dma(4),
        ],
        compiler_params=pltpu.CompilerParams(
            collective_id=0, has_side_effects=True, vmem_limit_bytes=limit
        ),
    )(centres, sample_idx.reshape(1, rows), coef.reshape(1, own), metric_factor)
    return pl.pallas_call(
        finish,
        out_shape=(
            jax.ShapeDtypeStruct((width // n, width), F32),
            jax.ShapeDtypeStruct((rows, width), F32),
        ),
        in_specs=[vmem] * 2,
        out_specs=(vmem, vmem),
        compiler_params=pltpu.CompilerParams(vmem_limit_bytes=40 * 2**20),
    )(gall, grads)


def solution(mesh):
    chips = mesh.shape["ctr"] // 2
    A = 1
    while A * A < chips:
        A *= 2
    B = chips // A
    placed = (P(("grp", "ctr"), None), P(("grp", "ctr")), P(("grp", "ctr")), P())
    return jax.shard_map(
        functools.partial(local, A, B),
        mesh=mesh,
        in_specs=placed,
        out_specs=(P(("grp", "ctr"), None), P(("grp", "ctr"), None)),
        check_vma=False,
    )
```
